512 devices in a mesh: dp: 32 (over y, x, core), tensor: 16 (over z).
Axes of the slice: x: 4, y: 4, z: 16, core: 2. Of those that a mesh axis runs over, the one named last changes fastest.
Arguments:
- hidden: bfloat16 [24576, 4096], P('dp', 'tensor'), may hold values from -4 to 4
- queries: bfloat16 [24576, 4096], P('dp', 'tensor')
- database: bfloat16 [1024, 128, 896], P('dp', 'tensor'), may hold values from -6 to 6
- w_key: bfloat16 [896, 4096], P(None, 'tensor'), may hold values from -0.1875 to 0.1875
- w_value: bfloat16 [896, 4096], P(None, 'tensor'), may hold values from -0.1875 to 0.1875
- w_out: bfloat16 [4096, 4096], P(None, 'tensor'), may hold values from -0.09375 to 0.09375
- owners: int32 [384, 2], P('dp'), may hold values from 0 to 31, all different within a row; in each aligned block of 12 rows (0 to 11, 12 to 23, ...) at most 2 rows name the same one
- entry_slots: int32 [384, 2], P('dp'), may hold values from 0 to 31
Outputs:
- mixed: bfloat16 [24576, 4096], P('dp', 'tensor')
The draws below stay inside these ranges and needn't reach their ends.
Inputs may be any that keep to these rules, and one draw needn't show every extreme that they name: Among the spans of one dp index (aligned blocks of 12 rows) no owner is named more than 2 times, a bound that some block reaches; the 2 neighbours of a span have different owners.
All inputs are finite; a program needn't handle non-finite values.
Results may differ from the reference program's by a relative error of at most 0.012.
The reference program's roundings to bfloat16 on the way count: a program that leaves them out, or rounds other values in their place, can miss the bound.
Values may be sent and summed in bfloat16 or wider, within the bound.
A program may use at most 64 MiB of HBM per device.

```python
import math
import jax
import jax.numpy as jnp
import numpy as np
from jax import lax

D = 4096
HEADS = 32
HEAD_DIM = 128
E = 896
SPAN = 64
NLEN = 128
NEIGH = 2
CH_DEV = 12
DB_DEV = 32
CAP = 2
SPANS = 384
TOKENS = 24576
DB = 1024
N_DP = 32


def draw_queries(key, part):
    first_key = jax.random.fold_in(jax.random.fold_in(key, 17), 0)
    values = jax.random.normal(first_key, (TOKENS, D), jnp.float32) * 3.0
    return values.astype(jnp.bfloat16)


def place_ends(result, own_key, smallest, top_value):
    shape = result.shape
    index_at = [jax.random.randint(jax.random.fold_in(own_key, axis), (), 0, shape[axis]) for axis in range(len(shape))]
    result = result.at[tuple(index_at)].set(smallest)
    longest = shape.index(max(shape))
    index_at[longest] = (index_at[longest] + 1) % shape[longest]
    return result.at[tuple(index_at)].set(top_value)


def block_scale(own_key, dims, shards, low, top_value):
    def one(axis_at, parts):
        steps = jax.random.uniform(jax.random.fold_in(jax.random.fold_in(own_key, 6), axis_at), (parts,), jnp.float32, low / len(shards), top_value / len(shards))
        return jnp.repeat(jnp.exp(steps), dims[axis_at] // parts).reshape((-1,) + (1,) * (len(dims) - axis_at - 1))

    loudness = one(*shards[0])
    for cut in shards[1:]:
        loudness = loudness * one(*cut)
    return loudness


def deal_out(rng, own, number, rows, amount, top, limit, lean):
    sequence = jax.random.permutation(rng, amount)
    heavy_load, usual = shares(amount, rows * top, limit, lean, True), shares(amount, rows * top, limit, lean, False)
    places = jnp.arange(amount)

    def named(tallies, rotation):
        used = int((tallies > 0).sum())
        fixed = max(1, used // 4)
        shifted = fixed + (places - fixed + rotation * (used - fixed)) % max(1, amount - fixed)
        return jnp.zeros((amount,), jnp.int32).at[sequence[jnp.where(places < fixed, places, shifted)]].set(jnp.asarray(tallies, jnp.int32))

    tallies = jnp.where(number % 4 == 0, named(heavy_load, number // 4), named(usual, number - number // 4 - 1))
    mixed = jax.random.permutation(jax.random.fold_in(own, 3), amount)
    donor, taker = mixed[0:amount // 2 * 2:2], mixed[1:amount // 2 * 2:2]
    room = jnp.minimum(tallies[donor] - 1, limit - tallies[taker]) // 2
    room = jnp.where((donor == sequence[0]) | (taker == sequence[0]) | (tallies[taker] == 0), 0, jnp.maximum(room, 0))
    shifted = jax.random.randint(jax.random.fold_in(own, 4), (amount // 2,), 0, 1 << 20) % (room + 1)
    tallies = tallies.at[donor].add(-shifted).at[taker].add(shifted)
    members = jnp.searchsorted(jnp.cumsum(tallies), jnp.arange(rows * top), side="right").astype(jnp.int32)
    grid = members.reshape(top, rows).T
    grid = grid[jax.random.permutation(jax.random.fold_in(own, 1), rows)]
    rotation = jax.random.randint(jax.random.fold_in(own, 2), (rows, 1), 0, top)
    return jnp.take_along_axis(grid, (jnp.arange(top)[None, :] + rotation) % top, axis=1)


def shares(amount, total, most, lean, full):
    portions = [(1 << 20) // math.isqrt(grade ** lean) + 1 for grade in range(1, amount + 1)]
    largest = most if full else min(most, max(-(-total // amount), total * portions[0] // sum(portions)))
    least = 1 if total - largest >= amount - 1 else 0
    given, surplus = [largest] + [least] * (amount - 1), total - largest - least * (amount - 1)
    while surplus > 0:
        candidates = [i for i in range(1, amount) if given[i] < largest] or [i for i in range(1, amount) if given[i] < most]
        mass, left = sum([portions[i] for i in candidates]), surplus
        for i in candidates:
            addition = min(most - given[i], max(1, left * portions[i] // mass), surplus)
            given[i] = given[i] + addition
            surplus = surplus - addition
    return np.array(given)


def gaussian(own_key, dims, spread, reach, cuts=(), dtype=jnp.bfloat16):
    values = jax.random.normal(own_key, dims, jnp.float32) * spread
    if len(cuts) > 0:
        values = block_scale(own_key, dims, cuts, -0.22, 0.18) * values
    return jnp.clip(values, min=-reach, max=reach).astype(dtype)


def setup_inputs(seed: int = 0) -> dict:
    arg_keys = jax.random.split(jax.random.key(seed), 9)
    hidden = gaussian(arg_keys[0], (TOKENS, D), 0.5, 4.0, ((0, 32), (1, 16)))
    queries = draw_queries(jax.random.fold_in(arg_keys[8], 71), 0)
    database = gaussian(arg_keys[2], (DB, NLEN, E), 1.0, 6.0, ((0, 32), (1, 16)))
    w_key = gaussian(arg_keys[3], (E, D), E ** -0.5, 0.1875, ((1, 16),))
    w_value = gaussian(arg_keys[4], (E, D), E ** -0.5, 0.1875, ((1, 16),))
    w_out = gaussian(arg_keys[5], (D, D), D ** -0.5, 0.09375, ((1, 16),))
    owners_keys = jax.random.split(jax.random.fold_in(arg_keys[6], 1), SPANS // CH_DEV)
    owners_turns = jax.random.permutation(jax.random.fold_in(arg_keys[6], 3), SPANS // CH_DEV)
    owners = jax.vmap(lambda own, number: deal_out(jax.random.fold_in(arg_keys[6], 2), own, number, CH_DEV, N_DP, NEIGH, CAP, 2))(owners_keys, owners_turns).reshape((SPANS, NEIGH))
    entry_slots = place_ends(jax.random.randint(arg_keys[7], (SPANS, NEIGH), 0, DB_DEV), jax.random.fold_in(arg_keys[7], 1), 0, DB_DEV - 1).astype(jnp.int32)
    return dict(hidden=hidden, queries=queries, database=database, w_key=w_key, w_value=w_value, w_out=w_out, owners=owners, entry_slots=entry_slots)


def reference(hidden, queries, database, w_key, w_value, w_out, owners, entry_slots):
    entries = (owners * DB_DEV + entry_slots).astype(jnp.int32)
    query_rows = queries.reshape(SPANS, SPAN, HEADS, HEAD_DIM)
    proj_weight = jnp.concatenate([w_key, w_value], axis=1)
    score_scale = 1.0 / math.sqrt(HEAD_DIM)

    def one_span(pair):
        span_query, span_ids = pair
        neighbours = jnp.take(database, span_ids, axis=0).reshape(NEIGH * NLEN, E)
        key_value = jnp.dot(neighbours, proj_weight, preferred_element_type=jnp.float32).astype(jnp.bfloat16)
        key_value = lax.optimization_barrier(key_value).astype(jnp.float32)
        key_rows = key_value[:, :D].reshape(NEIGH * NLEN, HEADS, HEAD_DIM)
        value_rows = key_value[:, D:].reshape(NEIGH * NLEN, HEADS, HEAD_DIM)
        scores = jnp.einsum('ihd,jhd->hij', span_query.astype(jnp.float32), key_rows) * score_scale
        row_max = lax.optimization_barrier(jnp.max(scores, axis=-1, keepdims=True))
        weights = jnp.exp(scores - row_max)
        weights = weights / lax.optimization_barrier(jnp.sum(weights, axis=-1, keepdims=True))
        softmax_low = lax.optimization_barrier(weights.astype(jnp.bfloat16)).astype(jnp.float32)
        attended = jnp.einsum('hij,jhd->ihd', softmax_low, value_rows)
        return attended.astype(jnp.bfloat16).reshape(SPAN, D)
    attended = lax.map(one_span, (query_rows, entries)).reshape(TOKENS, D)
    projected = jnp.dot(attended, w_out, preferred_element_type=jnp.float32)
    return (hidden.astype(jnp.float32) + projected).astype(jnp.bfloat16)
```

```python
import functools
import math

import jax
import jax.numpy as jnp
from jax import lax
from jax.experimental import pallas as pl
from jax.experimental.pallas import tpu as pltpu
from jax.sharding import PartitionSpec as P

MESH = pl.DeviceIdType.MESH
BF = jnp.bfloat16
F32 = jnp.float32
NP = 12
PIECE = 128


def where_am_i():
    dp = lax.axis_index("dp")
    z = lax.axis_index("tensor")
    y = dp // 8
    x = lax.rem(dp // 2, 4)
    c = lax.rem(dp, 2)
    return dp, z, y, x, c, 2 * y + c


def dp_of(x, j):
    return (j // 2) * 8 + x * 2 + lax.rem(j, 2)


def turn(j, p):
    return lax.rem(p // 4 + j, 4)


def has_span(j, p):
    return turn(j, p) < 3


def slot_of(j, p):
    return (j // 4) * 3 + turn(j, p)


def span_of(j, p):
    return 4 * turn(j, p) + lax.rem(p, 4)


def plane_of(j, k):
    return 4 * lax.rem(k // 4 - j + 8, 4) + lax.rem(k, 4)


def remote(src, dst, ssem, rsem, dp, z):
    return pltpu.make_async_remote_copy(
        src_ref=src, dst_ref=dst, send_sem=ssem, recv_sem=rsem,
        device_id=(dp, z), device_id_type=MESH,
    )


def loop(lo, hi, body):
    def step(i, carry):
        body(i)
        return carry

    lax.fori_loop(lo, hi, step, 0)


def gather_yc(view, here, ssem, rsem, good, half):
    dp, z, y, x, c, j = here

    def at(dy, dc):
        return 2 * lax.rem(y + dy + 4, 4) + lax.rem(c + dc, 2)

    def send(block, part, target, number):
        return remote(view(block, part), view(block, part), ssem.at[number, part],
                      rsem.at[block, part], dp_of(x, target), z)

    up, down, twin, far = at(1, 0), at(-1, 0), at(0, 1), at(2, 0)
    if half is not None:

        @pl.when(good(j))
        def _():
            send(j, half, up, 0).start()
            send(j, half, down, 1).start()
            send(j, half, twin, 2).start()

        return None

    def forward():
        for part in (0, 1):

            @pl.when(good(down))
            def _():
                send(down, part, j, 0).wait_recv()
                if part == 0:
                    send(down, part, up, 6).start()
                send(down, part, twin, 3).start()

            @pl.when(good(up))
            def _():
                send(up, part, j, 0).wait_recv()
                if part == 1:
                    send(up, part, down, 6).start()
                send(up, part, twin, 4).start()

        for part in (0, 1):

            @pl.when(good(far))
            def _():
                send(far, part, j, 0).wait_recv()
                send(far, part, twin, 5).start()

    def finish():
        for part in (0, 1):
            for dy in (0, 1, 3, 2):
                other = at(dy, 1)

                @pl.when(good(other))
                def _():
                    send(other, part, j, 0).wait_recv()

            @pl.when(good(j))
            def _():
                for number in (0, 1, 2):
                    send(j, part, twin, number).wait_send()

            for number, block in ((3, down), (4, up), (5, far)):

                @pl.when(good(block))
                def _():
                    send(block, part, twin, number).wait_send()

        @pl.when(good(down))
        def _():
            send(down, 0, up, 6).wait_send()

        @pl.when(good(up))
        def _():
            send(up, 1, down, 6).wait_send()

    return forward, finish


def fetch_kernel(req_ref, sel_ref, db_ref, q_ref, w_ref, near_ref, q6_ref, wall_ref,
                 qa, rall, served, replies, mine,
                 rs, rr, qs, qr, q2s, q2r, as_, ar, ns, nr, gs, gr, zs, zr, xs, xr, fs, fr, lsem):
    here = where_am_i()
    dp, z, y, x, c, j = here
    barrier = pltpu.get_barrier_semaphore()

    def greet(i):
        pl.semaphore_signal(barrier, inc=1, device_id=(lax.rem(dp + i, 32), z), device_id_type=MESH)

    def greet_z(i):
        pl.semaphore_signal(barrier, inc=1, device_id=(dp, lax.rem(z + i, 16)), device_id_type=MESH)

    loop(1, 32, greet)
    loop(1, 16, greet_z)
    pl.semaphore_wait(barrier, 46)

    def req_copy(source, target):
        return remote(req_ref, rall.at[source], rs.at[target], rr.at[source], target, z)

    loop(1, 32, lambda i: req_copy(dp, lax.rem(dp + i, 32)).start())

    d = lax.rem(z - j + 16, 16)
    e, s = lax.rem(d, 8), d // 8
    right, left = lax.rem(z + 1, 16), lax.rem(z + 15, 16)
    xright, xleft = lax.rem(x + 1, 4), lax.rem(x + 3, 4)

    def wz(h, i, to, way):
        return remote(wall_ref.at[h, x, i], wall_ref.at[h, x, i], zs.at[way, i], zr.at[h, i], dp, to)

    def wx(h, i, way):
        return remote(wall_ref.at[h, x, i], wall_ref.at[h, x, i], xs.at[way, h, i], xr.at[way, h, i],
                      dp_of(xright if way == 0 else xleft, j), z)

    def wx_in(h, i, way):
        chunk = xleft if way == 0 else xright
        return remote(wall_ref.at[h, chunk, i], wall_ref.at[h, chunk, i], fs.at[h, i], xr.at[way, h, i],
                      dp_of(xright, j), z)

    def wf(h, i, way):
        chunk = xleft if way == 0 else xright
        return remote(wall_ref.at[h, chunk, i], wall_ref.at[h, chunk, i], fs.at[h, i], fr.at[h, i],
                      dp_of(xright if way == 0 else xleft, j), z)

    @pl.when(e == 0)
    def _():
        own = pltpu.make_async_copy(w_ref, wall_ref.at[s, x], lsem.at[0])
        own.start()
        own.wait()

        def inject(i):
            wz(s, i, right, 0).start()
            wz(s, i, left, 1).start()

        loop(0, NP, inject)

    def q_copy(k):
        p = plane_of(j, k)
        return p, remote(q_ref.at[k], qa.at[z // 8, lax.rem(z, 8)], qs.at[k],
                         qr.at[z], dp, p)

    def q_local(k):
        return pltpu.make_async_copy(q_ref.at[k], qa.at[z // 8, lax.rem(z, 8)], lsem.at[1])

    def q_send(k):
        p, copy = q_copy(k)

        @pl.when(p == z)
        def _():
            q_local(k).start()

        @pl.when(p != z)
        def _():
            copy.start()

    loop(0, 12, q_send)

    def slot(t):
        ia = t - e
        ib = t - 8 + e

        @pl.when((ia >= 0) & (ia < NP))
        def _():
            @pl.when(e > 0)
            def _():
                wz(s, ia, z, 0).wait_recv()
                wz(s, ia, right, 0).start()

            wx(s, ia, 0).start()
            wx(s, ia, 1).start()

        @pl.when((ib >= 0) & (ib < NP))
        def _():
            wz(1 - s, ib, z, 0).wait_recv()

            @pl.when(e >= 2)
            def _():
                wz(1 - s, ib, left, 1).start()

            wx(1 - s, ib, 0).start()
            wx(1 - s, ib, 1).start()

        for h, i in ((s, ia - 2), (1 - s, ib - 2)):

            @pl.when((i >= 0) & (i < NP))
            def _():
                wx_in(h, i, 0).wait_recv()
                wx_in(h, i, 1).wait_recv()

                @pl.when(lax.rem(i, 2) == 0)
                def _():
                    wf(h, i, 0).start()

                @pl.when(lax.rem(i, 2) == 1)
                def _():
                    wf(h, i, 1).start()

    rall[dp] = req_ref[...]
    loop(1, 32, lambda i: req_copy(lax.rem(dp + i, 32), dp).wait_recv())
    table = rall[:, 0, :].astype(F32).astype(BF)
    expand = (lax.broadcasted_iota(jnp.int32, (512, 32), 0) // 16
              == lax.broadcasted_iota(jnp.int32, (512, 32), 1)).astype(F32).astype(BF)
    spread = jnp.dot(expand, table, preferred_element_type=F32)
    row = lax.broadcasted_iota(jnp.int32, (512, 128), 0)
    lane = lax.broadcasted_iota(jnp.int32, (512, 128), 1)
    entry = jnp.sum(jnp.where(lane == 2 * dp + (row // 8) % 2, spread, 0.0), axis=1, keepdims=True)
    row = lax.broadcasted_iota(jnp.int32, (512, 256), 0)
    column = lax.broadcasted_iota(jnp.int32, (512, 256), 1)
    hot = ((column // 8 + 1).astype(F32) == entry) & (column % 8 == row % 8)
    picked = jnp.dot(hot.astype(F32).astype(BF), db_ref[...], preferred_element_type=F32)
    served[...] = picked.astype(BF).reshape(32, 16, 896)

    def reply(source, target):
        return remote(served.at[target], replies.at[source], as_.at[target], ar.at[source], target, z)

    loop(1, 32, lambda i: reply(dp, lax.rem(dp + i, 32)).start())
    loop(0, 5, slot)
    replies[dp] = served[dp]
    loop(1, 32, lambda i: reply(lax.rem(dp + i, 32), dp).wait_recv())
    got = jnp.dot(sel_ref[...], replies[...].reshape(512, 896), preferred_element_type=F32)
    mine[...] = got.astype(BF).reshape(12, 16, 896)

    def n_copy(k):
        p = plane_of(j, k)
        return p, remote(mine.at[k], near_ref.at[slot_of(j, p), z], ns.at[k], nr.at[z], dp, p)

    def n_local(k):
        return pltpu.make_async_copy(mine.at[k], near_ref.at[slot_of(j, z), z], lsem.at[2])

    def n_send(k):
        p, copy = n_copy(k)

        @pl.when(p == z)
        def _():
            n_local(k).start()

        @pl.when(p != z)
        def _():
            copy.start()

    loop(0, 12, n_send)
    loop(5, 9, slot)

    def q2(source, target):
        return remote(qa.at[:, target], q6_ref.at[slot_of(source, z)], q2s.at[target], q2r.at[source],
                      dp_of(x, target), z)

    def q2_local():
        return pltpu.make_async_copy(qa.at[:, j], q6_ref.at[slot_of(j, z)], lsem.at[3])

    @pl.when(has_span(j, z))
    def _():
        q_local(0).wait()
        loop(1, 16, lambda i: remote(q_ref.at[0], qa.at[0, 0], qs.at[0], qr.at[lax.rem(z + i, 16)],
                                     dp, z).wait_recv())
        q2_local().start()
        loop(1, 8, lambda i: q2(j, lax.rem(j + i, 8)).start())

    loop(9, 11, slot)

    def view(block, part):
        return near_ref.at[slot_of(block, z), pl.ds(part * 8, 8)]

    def good(block):
        return has_span(block, z)

    @pl.when(good(j))
    def _():
        n_local(0).wait()
        loop(1, 16, lambda i: remote(mine.at[0], near_ref.at[0, 0], ns.at[0], nr.at[lax.rem(z + i, 16)],
                                     dp, z).wait_recv())

    for part in (0, 1):
        gather_yc(view, here, gs, gr, good, part)
    loop(11, 13, slot)
    forward, finish = gather_yc(view, here, gs, gr, good, None)
    forward()
    loop(13, 22, slot)

    finish()

    @pl.when(has_span(j, z))
    def _():
        q2_local().wait()
        loop(1, 8, lambda i: q2(j, lax.rem(j + i, 8)).wait_send())

    def q2_wait(i):
        other = lax.rem(j + i, 8)

        @pl.when(has_span(other, z))
        def _():
            q2(other, j).wait_recv()

    loop(1, 8, q2_wait)

    def sent(k):
        p, copy = n_copy(k)
        _, copy_q = q_copy(k)

        @pl.when(p != z)
        def _():
            copy.wait_send()
            copy_q.wait_send()

    loop(0, 12, sent)

    def sent_dp(i):
        other = lax.rem(dp + i, 32)
        req_copy(dp, other).wait_send()
        reply(dp, other).wait_send()

    loop(1, 32, sent_dp)

    def sent_w(i):
        @pl.when(e >= 0)
        def _():
            wz(s, i, right, 0).wait_send()

        @pl.when(e == 0)
        def _():
            wz(s, i, left, 1).wait_send()

        @pl.when(e >= 2)
        def _():
            wz(1 - s, i, left, 1).wait_send()

        for h in (0, 1):
            wx(h, i, 0).wait_send()
            wx(h, i, 1).wait_send()
            wf(h, i, 0).wait_send()
            wf(h, i, 0).wait_recv()

    loop(0, NP, sent_w)


def attend_kernel(near_ref, q_ref, wall_ref, hid_ref, out_ref,
                  near, wk, wv, wo, att, acc, res, ob, fb,
                  ls, gs, gr, bs, br, cs, cr, lsem):
    here = where_am_i()
    dp, z, y, x, c, j = here
    loads = []

    def load(src, dst, number):
        copy = pltpu.make_async_copy(src, dst, ls.at[number])
        copy.start()
        loads.append(copy)

    for h in (0, 1):
        for chunk in range(4):
            load(wall_ref.at[h, chunk, pl.ds(0, 224)], wk.at[h, pl.ds(224 * chunk, 224)], 16 * h + 4 * chunk)
            load(wall_ref.at[h, chunk, pl.ds(224, 224)], wv.at[h, pl.ds(224 * chunk, 224)],
                 16 * h + 4 * chunk + 1)
    load(near_ref, near, 32)
    first = len(loads)
    for h in (0, 1):
        for chunk in range(4):
            load(wall_ref.at[h, chunk, pl.ds(512, 1024)], wo.at[h, pl.ds(1024 * chunk, 1024)],
                 16 * h + 4 * chunk + 2)

    barrier = pltpu.get_barrier_semaphore()
    loop(1, 8, lambda i: pl.semaphore_signal(
        barrier, inc=1, device_id=(dp_of(x, lax.rem(j + i, 8)), z), device_id_type=MESH))
    loop(1, 16, lambda i: pl.semaphore_signal(
        barrier, inc=1, device_id=(dp, lax.rem(z + i, 16)), device_id_type=MESH))
    pl.semaphore_wait(barrier, 22)
    for copy in loads[:first]:
        copy.wait()

    scale = 1.0 / math.sqrt(128)

    def span(n):
        rows = near[n]
        for h in (0, 1):
            keys = jnp.dot(rows, wk[h], preferred_element_type=F32).astype(BF)
            values = jnp.dot(rows, wv[h], preferred_element_type=F32).astype(BF)
            for m in (0, 1):
                cut = slice(128 * m, 128 * m + 128)
                scores = lax.dot_general(q_ref[n, h, :, cut], keys[:, cut], (((1,), (1,)), ((), ())),
                                         preferred_element_type=F32) * scale
                w = jnp.exp(scores - jnp.max(scores, axis=-1, keepdims=True))
                w = w / jnp.sum(w, axis=-1, keepdims=True)
                o = jnp.dot(w.astype(BF), values[:, cut], preferred_element_type=F32)
                att[j, n, :, 256 * h + 128 * m:256 * h + 128 * m + 128] = o.astype(BF)

    def view(block, part):
        return att.at[block, pl.ds(3 * part, 3)]

    def good(block):
        return block >= 0

    for part in (0, 1):
        loop(3 * part, 3 * part + 3, span)
        gather_yc(view, here, gs, gr, good, part)
    forward, finish = gather_yc(view, here, gs, gr, good, None)
    forward()
    finish()
    for copy in loads[first:]:
        copy.wait()

    acc[...] = jnp.zeros_like(acc)

    def project(b):
        rows = att[b].reshape(384, 512)
        for g in (0, 1):
            total = acc[g]
            for h in (0, 1):
                w = wo[g, pl.ds(pl.multiple_of((b + 8 * h) * 256, 256), 256), :]
                total = total + jnp.dot(rows[:, 256 * h:256 * h + 256], w, preferred_element_type=F32)
            acc[g] = total

    loop(0, 8, project)
    for g in (0, 1):
        res[:, g] = acc[g].astype(BF).reshape(6, 64, 256)

    def b_copy(source, target):
        return remote(res.at[slot_of(target, z)], ob.at[source], bs.at[target], br.at[source],
                      dp_of(x, target), z)

    def b_send(i):
        other = lax.rem(j + i, 8)

        @pl.when(has_span(other, z))
        def _():
            b_copy(j, other).start()

    loop(1, 8, b_send)

    def c_copy(source, h, k):
        to = source + 8 * h
        return to, remote(ob.at[source, h], fb.at[k], cs.at[to], cr.at[k], dp, to)

    def c_local(source, h, k):
        return pltpu.make_async_copy(ob.at[source, h], fb.at[k], lsem.at[0])

    def c_send(source):
        for h in (0, 1):
            to, copy = c_copy(source, h, span_of(j, z))

            @pl.when(to == z)
            def _():
                c_local(source, h, span_of(j, z)).start()

            @pl.when(to != z)
            def _():
                copy.start()

    @pl.when(has_span(j, z))
    def _():
        ob[j] = res[slot_of(j, z)]
        c_send(j)

        def relay(i):
            other = lax.rem(j + i, 8)
            b_copy(other, j).wait_recv()
            c_send(other)

        loop(1, 8, relay)
        c_local(0, 0, 0).wait()

    def land(k):
        @pl.when(plane_of(j, k) != z)
        def _():
            remote(ob.at[0, 0], fb.at[k], cs.at[0], cr.at[k], dp, z).wait_recv()

        out_ref[k] = (hid_ref[k].astype(F32) + fb[k].astype(F32)).astype(BF)

    loop(0, 12, land)

    def b_sent(i):
        other = lax.rem(j + i, 8)

        @pl.when(has_span(other, z))
        def _():
            b_copy(j, other).wait_send()

    loop(1, 8, b_sent)

    @pl.when(has_span(j, z))
    def _():
        def c_sent(i):
            to = lax.rem(z + i, 16)
            remote(ob.at[0, 0], fb.at[0], cs.at[to], cr.at[0], dp, to).wait_send()

        loop(1, 16, c_sent)


def fetch(requests, sel, db, queries, weights):
    dma = pltpu.SemaphoreType.DMA
    any_ = pl.BlockSpec(memory_space=pl.ANY)
    vmem = pl.BlockSpec(memory_space=pltpu.VMEM)
    return pl.pallas_call(
        fetch_kernel,
        name="fetch",
        out_shape=(
            jax.ShapeDtypeStruct((6, 16, 16, 896), BF),
            jax.ShapeDtypeStruct((6, 2, 64, 256), BF),
            jax.ShapeDtypeStruct((2, 4, NP, PIECE, 256), BF),
        ),
        in_specs=[vmem, vmem, vmem, any_, any_],
        out_specs=(any_, any_, any_),
        scratch_shapes=[
            pltpu.VMEM((2, 8, 64, 256), BF),
            pltpu.VMEM((32, 8, 128), jnp.int32),
            pltpu.VMEM((32, 16, 896), BF),
            pltpu.VMEM((32, 16, 896), BF),
            pltpu.VMEM((12, 16, 896), BF),
            dma((32,)), dma((32,)),
            dma((12,)), dma((16,)),
            dma((8,)), dma((8,)),
            dma((32,)), dma((32,)),
            dma((12,)), dma((16,)),
            dma((7, 2)), dma((8, 2)),
            dma((2, NP)), dma((2, NP)),
            dma((2, 2, NP)), dma((2, 2, NP)),
            dma((2, NP)), dma((2, NP)),
            dma((4,)),
        ],
        compiler_params=pltpu.CompilerParams(
            collective_id=0, has_side_effects=True, vmem_limit_bytes=32 * 2**20
        ),
    )(requests, sel, db, queries, weights)


def attend(near, q6, wall, hidden):
    dma = pltpu.SemaphoreType.DMA
    any_ = pl.BlockSpec(memory_space=pl.ANY)
    vmem = pl.BlockSpec(memory_space=pltpu.VMEM)
    return pl.pallas_call(
        attend_kernel,
        name="attend",
        out_shape=jax.ShapeDtypeStruct((12, 64, 256), BF),
        in_specs=[any_, vmem, any_, vmem],
        out_specs=vmem,
        scratch_shapes=[
            pltpu.VMEM((6, 256, 896), BF),
            pltpu.VMEM((2, 896, 256), BF),
            pltpu.VMEM((2, 896, 256), BF),
            pltpu.VMEM((2, 4096, 256), BF),
            pltpu.VMEM((8, 6, 64, 512), BF),
            pltpu.VMEM((2, 384, 256), F32),
            pltpu.VMEM((6, 2, 64, 256), BF),
            pltpu.VMEM((8, 2, 64, 256), BF),
            pltpu.VMEM((12, 64, 256), BF),
            dma((33,)),
            dma((7, 2)), dma((8, 2)),
            dma((8,)), dma((8,)),
            dma((16,)), dma((12,)),
            dma((1,)),
        ],
        compiler_params=pltpu.CompilerParams(
            collective_id=1, has_side_effects=True, vmem_limit_bytes=40 * 2**20
        ),
    )(near, q6, wall, hidden)


def per_device(hidden, queries, database, w_key, w_value, w_out, owners, entry_slots):
    x = lax.rem(lax.axis_index("dp") // 2, 4)
    wanted = owners.reshape(-1)
    slots = entry_slots.reshape(-1)
    number = jnp.arange(24, dtype=jnp.int32)
    same = (wanted[:, None] == wanted[None, :]) & (number[None, :] < number[:, None])
    order = jnp.sum(same.astype(jnp.int32), axis=1)
    position = wanted * 2 + order
    placed = position[:, None] == jnp.arange(128, dtype=jnp.int32)[None, :]
    requests = jnp.sum(jnp.where(placed, (slots + 1)[:, None], 0), axis=0)
    requests = jnp.broadcast_to(requests[None, :], (8, 128))
    token = jnp.arange(8, dtype=jnp.int32)
    source = (position[:, None] * 8 + token[None, :]).reshape(192, 1)
    sel = (source == jnp.arange(512, dtype=jnp.int32)[None, :]).astype(BF)
    take = lambda w, n: lax.dynamic_slice(w, (x * n, 0), (n, 256))
    weights = jnp.concatenate(
        [take(w_key, 224), take(w_value, 224), jnp.zeros((64, 256), BF), take(w_out, 1024)], axis=0
    )
    near, q6, wall = fetch(
        requests, sel, database.reshape(256, 896), queries.reshape(12, 64, 256),
        weights.reshape(NP, PIECE, 256),
    )
    mixed = attend(
        near.reshape(6, 256, 896), q6, wall.reshape(2, 4, NP * PIECE, 256), hidden.reshape(12, 64, 256)
    )
    return mixed.reshape(768, 256)


def solution(mesh):
    in_specs = (
        P("dp", "tensor"),
        P("dp", "tensor"),
        P("dp", "tensor", None),
        P(None, "tensor"),
        P(None, "tensor"),
        P(None, "tensor"),
        P("dp", None),
        P("dp", None),
    )
    return jax.shard_map(
        per_device, mesh=mesh, in_specs=in_specs, out_specs=P("dp", "tensor"), check_vma=False
    )
```

```python
import functools
import math

import jax
import jax.numpy as jnp
from jax import lax
from jax.experimental import pallas as pl
from jax.experimental.pallas import tpu as pltpu
from jax.sharding import PartitionSpec as P

MESH = pl.DeviceIdType.MESH
BF = jnp.bfloat16
F32 = jnp.float32
NP = 12
NKV = 4
PIECE = 128
SKEW = 1
LAG = 2
LAST = NP + 8 * SKEW + LAG
PACE = dict(ask=2, fetch=4, move=4, near=2, near_step=1, span=1, att_step=1)


def where_am_i():
    dp = lax.axis_index("dp")
    z = lax.axis_index("tensor")
    y = dp // 8
    x = lax.rem(dp // 2, 4)
    c = lax.rem(dp, 2)
    return dp, z, y, x, c, 2 * y + c


def dp_of(x, j):
    return (j // 2) * 8 + x * 2 + lax.rem(j, 2)


def turn(j, p):
    return lax.rem(p // 4 + j, 4)


def has_span(j, p):
    return turn(j, p) < 3


def slot_of(j, p):
    return (j // 4) * 3 + turn(j, p)


def span_of(j, p):
    return 4 * turn(j, p) + lax.rem(p, 4)


def plane_of(j, k):
    return 4 * lax.rem(k // 4 - j + 8, 4) + lax.rem(k, 4)


def remote(src, dst, ssem, rsem, dp, z):
    return pltpu.make_async_remote_copy(
        src_ref=src, dst_ref=dst, send_sem=ssem, recv_sem=rsem,
        device_id=(dp, z), device_id_type=MESH,
    )


def loop(lo, hi, body):
    def step(i, carry):
        body(i)
        return carry

    lax.fori_loop(lo, hi, step, 0)


def gather_yc(view, here, ssem, rsem, good, half, between=None):
    dp, z, y, x, c, j = here

    def at(dy, dc):
        return 2 * lax.rem(y + dy + 4, 4) + lax.rem(c + dc, 2)

    def send(block, part, target, number):
        return remote(view(block, part), view(block, part), ssem.at[number, part],
                      rsem.at[block, part], dp_of(x, target), z)

    up, down, twin, far = at(1, 0), at(-1, 0), at(0, 1), at(2, 0)
    if half is not None:

        @pl.when(good(j))
        def _():
            send(j, half, up, 0).start()
            send(j, half, down, 1).start()
            send(j, half, twin, 2).start()

        return None

    def forward():
        for part in (0, 1):

            @pl.when(good(down))
            def _():
                send(down, part, j, 0).wait_recv()
                if part == 0:
                    send(down, part, up, 6).start()
                send(down, part, twin, 3).start()

            @pl.when(good(up))
            def _():
                send(up, part, j, 0).wait_recv()
                if part == 1:
                    send(up, part, down, 6).start()
                send(up, part, twin, 4).start()

            between()

        for part in (0, 1):

            @pl.when(good(far))
            def _():
                send(far, part, j, 0).wait_recv()
                send(far, part, twin, 5).start()

            between()

    def finish():
        for part in (0, 1):
            for dy in (0, 1, 3, 2):
                other = at(dy, 1)

                @pl.when(good(other))
                def _():
                    send(other, part, j, 0).wait_recv()

            @pl.when(good(j))
            def _():
                for number in (0, 1, 2):
                    send(j, part, twin, number).wait_send()

            for number, block in ((3, down), (4, up), (5, far)):

                @pl.when(good(block))
                def _():
                    send(block, part, twin, number).wait_send()

        @pl.when(good(down))
        def _():
            send(down, 0, up, 6).wait_send()

        @pl.when(good(up))
        def _():
            send(up, 1, down, 6).wait_send()

    return forward, finish


def layer_kernel(own_ref, ent_ref, db_hbm, q_ref, wk_ref, wv_ref, wo_ref, hid_hbm, out_ref,
                 db_ref, hid_ref, req_ref, qa, q6, rall, served, replies, mine, near, wall, att, acc, res, ob, fb,
                 rs, rr, qs, qr, q2s, q2r, as_, ar, ns, nr, gs, gr,
                 wl, zs, zr, xs, xr, fs, fr, ts, tr, bs, br, cs, cr, lsem, load):
    here = where_am_i()
    dp, z, y, x, c, j = here
    d = lax.rem(z - j + 16, 16)
    e, s = lax.rem(d, 8), d // 8
    right, left = lax.rem(z + 1, 16), lax.rem(z + 15, 16)
    xright, xleft = lax.rem(x + 1, 4), lax.rem(x + 3, 4)

    def piece(h, i, chunk):
        return wall.at[h, pl.ds(pl.multiple_of((4 * i + chunk) * PIECE, PIECE), PIECE)]

    load_db = pltpu.make_async_copy(db_hbm, db_ref, load.at[0])
    load_hid = pltpu.make_async_copy(hid_hbm, hid_ref, load.at[1])
    load_db.start()

    def own_rows(ref, g):
        return ref.at[pl.ds(pl.multiple_of(g * PIECE, PIECE), PIECE)]

    def own(i, ref, g):
        return pltpu.make_async_copy(own_rows(ref, g), piece(s, i, x), wl.at[i])

    @pl.when(e == 0)
    def _():
        for i in range(NKV):
            g = 4 * i + x

            @pl.when(g < 7)
            def _():
                own(i, wk_ref, jnp.minimum(g, 6)).start()

            @pl.when(g >= 7)
            def _():
                own(i, wv_ref, jnp.clip(g - 7, 0, 6)).start()

        for i in range(NKV, NP):
            own(i, wo_ref, 4 * (i - NKV) + x).start()

    load_hid.start()
    barrier = pltpu.get_barrier_semaphore()

    def greet(i):
        pl.semaphore_signal(barrier, inc=1, device_id=(lax.rem(dp + i, 32), z), device_id_type=MESH)

    def greet_z(i):
        pl.semaphore_signal(barrier, inc=1, device_id=(dp, lax.rem(z + i, 16)), device_id_type=MESH)

    loop(1, 32, greet)
    loop(1, 16, greet_z)
    pl.semaphore_wait(barrier, 46)

    number = lax.broadcasted_iota(jnp.int32, (24, 12), 0)
    lane = lax.broadcasted_iota(jnp.int32, (24, 12), 1)

    def column(ref):
        both = jnp.where(number < 12, ref[0:1, :], ref[1:2, :])
        return jnp.sum(jnp.where(lane == number % 12, both, 0), axis=1, keepdims=True)

    wanted = column(own_ref)
    order = jnp.zeros((24, 1), jnp.int32)
    for n in (0, 1):
        earlier = (own_ref[n:n + 1, :] == wanted) & (lane + 12 * n < number)
        order = order + jnp.sum(earlier.astype(jnp.int32), axis=1, keepdims=True)
    placed = (2 * wanted + order) == lax.broadcasted_iota(jnp.int32, (24, 128), 1)
    row = jnp.sum(jnp.where(placed, column(ent_ref) + 1, 0), axis=0, keepdims=True)
    req_ref[...] = jnp.broadcast_to(row, (8, 128))

    def req_copy(source, target):
        return remote(req_ref, rall.at[source], rs.at[target], rr.at[source], target, z)

    loop(1, 32, lambda i: req_copy(dp, lax.rem(dp + i, 32)).start())

    def wz(h, i, to, way):
        return remote(piece(h, i, x), piece(h, i, x), zs.at[way, i], zr.at[h, i], dp, to)

    def wx(h, i, way):
        return remote(piece(h, i, x), piece(h, i, x), xs.at[way, h, i], xr.at[way, h, i],
                      dp_of(xright if way == 0 else xleft, j), z)

    def wx_in(h, i, way):
        chunk = xleft if way == 0 else xright
        return remote(piece(h, i, chunk), piece(h, i, chunk), fs.at[h, i], xr.at[way, h, i],
                      dp_of(xright, j), z)

    def wf(h, i, way):
        chunk = xleft if way == 0 else xright
        return remote(piece(h, i, chunk), piece(h, i, chunk), fs.at[h, i], fr.at[h, i],
                      dp_of(xright if way == 0 else xleft, j), z)

    def inject(lo, hi):
        @pl.when(e == 0)
        def _():
            def one(i):
                own(i, wo_ref, 0).wait()
                wz(s, i, right, 0).start()
                wz(s, i, left, 1).start()

            loop(lo, hi, one)

    inject(0, NP)

    def q_copy(k):
        p = plane_of(j, k)
        return p, remote(q_ref.at[k], qa.at[z // 8, lax.rem(z, 8)], qs.at[k],
                         qr.at[z], dp, p)

    def q_local(k):
        return pltpu.make_async_copy(q_ref.at[k], qa.at[z // 8, lax.rem(z, 8)], lsem.at[1])

    def q_send(k):
        p, copy = q_copy(k)

        @pl.when(p == z)
        def _():
            q_local(k).start()

        @pl.when(p != z)
        def _():
            copy.start()

    loop(0, 12, q_send)

    def slot(t):
        ia = t - SKEW * e
        ib = t - SKEW * (8 - e)

        @pl.when((ia >= 0) & (ia < NP))
        def _():
            @pl.when(e > 0)
            def _():
                wz(s, ia, z, 0).wait_recv()
                wz(s, ia, right, 0).start()

            wx(s, ia, 0).start()
            wx(s, ia, 1).start()

        @pl.when((ib >= 0) & (ib < NP))
        def _():
            wz(1 - s, ib, z, 0).wait_recv()

            @pl.when(e >= 2)
            def _():
                wz(1 - s, ib, left, 1).start()

            wx(1 - s, ib, 0).start()
            wx(1 - s, ib, 1).start()

        for h, i in ((s, ia - LAG), (1 - s, ib - LAG)):

            @pl.when((i >= 0) & (i < NP))
            def _():
                wx_in(h, i, 0).wait_recv()
                wx_in(h, i, 1).wait_recv()

                @pl.when(lax.rem(i, 2) == 0)
                def _():
                    wf(h, i, 0).start()

                @pl.when(lax.rem(i, 2) == 1)
                def _():
                    wf(h, i, 1).start()

    done = [0]

    def slots(count):
        upto = min(done[0] + count, LAST)
        if upto > done[0]:
            loop(done[0], upto, slot)
        done[0] = upto

    slots(PACE["ask"])

    rall[dp] = req_ref[...]
    loop(1, 32, lambda i: req_copy(lax.rem(dp + i, 32), dp).wait_recv())
    load_db.wait()
    table = rall[:, 0, :].astype(F32).astype(BF)
    expand = (lax.broadcasted_iota(jnp.int32, (512, 32), 0) // 16
              == lax.broadcasted_iota(jnp.int32, (512, 32), 1)).astype(F32).astype(BF)
    spread = jnp.dot(expand, table, preferred_element_type=F32)
    row = lax.broadcasted_iota(jnp.int32, (512, 128), 0)
    lane = lax.broadcasted_iota(jnp.int32, (512, 128), 1)
    entry = jnp.sum(jnp.where(lane == 2 * dp + (row // 8) % 2, spread, 0.0), axis=1, keepdims=True)
    row = lax.broadcasted_iota(jnp.int32, (512, 256), 0)
    column = lax.broadcasted_iota(jnp.int32, (512, 256), 1)
    hot = ((column // 8 + 1).astype(F32) == entry) & (column % 8 == row % 8)
    picked = jnp.dot(hot.astype(F32).astype(BF), db_ref[...], preferred_element_type=F32)
    served[...] = picked.astype(BF).reshape(32, 16, 896)

    def reply(source, target):
        return remote(served.at[target], replies.at[source], as_.at[target], ar.at[source], target, z)

    loop(1, 32, lambda i: reply(dp, lax.rem(dp + i, 32)).start())
    r = lax.broadcasted_iota(jnp.int32, (192, 24), 0)
    request = lax.broadcasted_iota(jnp.int32, (192, 24), 1) == 12 * ((r // 8) % 2) + r // 16
    spread = jnp.dot(request.astype(F32).astype(BF), placed.astype(F32).astype(BF), preferred_element_type=F32)
    widen = (lax.broadcasted_iota(jnp.int32, (128, 512), 1) // 8
             == lax.broadcasted_iota(jnp.int32, (128, 512), 0))
    spread = jnp.dot(spread.astype(BF), widen.astype(F32).astype(BF), preferred_element_type=F32)
    token = (lax.broadcasted_iota(jnp.int32, (192, 512), 0) % 8
             == lax.broadcasted_iota(jnp.int32, (192, 512), 1) % 8)
    sel = jnp.where(token, spread, 0.0).astype(BF)
    slots(PACE["fetch"])
    replies[dp] = served[dp]
    loop(1, 32, lambda i: reply(lax.rem(dp + i, 32), dp).wait_recv())
    got = jnp.dot(sel, replies[...].reshape(512, 896), preferred_element_type=F32)
    mine[...] = got.astype(BF).reshape(12, 16, 896)

    def n_copy(k):
        p = plane_of(j, k)
        return p, remote(mine.at[k], near.at[slot_of(j, p), z], ns.at[k], nr.at[z], dp, p)

    def n_local(k):
        return pltpu.make_async_copy(mine.at[k], near.at[slot_of(j, z), z], lsem.at[2])

    def n_send(k):
        p, copy = n_copy(k)

        @pl.when(p == z)
        def _():
            n_local(k).start()

        @pl.when(p != z)
        def _():
            copy.start()

    loop(0, 12, n_send)
    slots(PACE["move"])

    def q2(source, target):
        return remote(qa.at[:, target], q6.at[slot_of(source, z)], q2s.at[target], q2r.at[source],
                      dp_of(x, target), z)

    def q2_local():
        return pltpu.make_async_copy(qa.at[:, j], q6.at[slot_of(j, z)], lsem.at[3])

    @pl.when(has_span(j, z))
    def _():
        q_local(0).wait()
        loop(1, 16, lambda i: remote(q_ref.at[0], qa.at[0, 0], qs.at[0], qr.at[lax.rem(z + i, 16)],
                                     dp, z).wait_recv())
        q2_local().start()
        loop(1, 8, lambda i: q2(j, lax.rem(j + i, 8)).start())


    def view(block, part):
        return near.at[slot_of(block, z), pl.ds(part * 8, 8)]

    def good(block):
        return has_span(block, z)

    @pl.when(good(j))
    def _():
        n_local(0).wait()
        loop(1, 16, lambda i: remote(mine.at[0], near.at[0, 0], ns.at[0], nr.at[lax.rem(z + i, 16)],
                                     dp, z).wait_recv())

    for part in (0, 1):
        gather_yc(view, here, gs, gr, good, part)
    slots(PACE["near"])
    forward, finish = gather_yc(view, here, gs, gr, good, None, lambda: slots(PACE["near_step"]))
    forward()
    finish()

    @pl.when(has_span(j, z))
    def _():
        q2_local().wait()
        loop(1, 8, lambda i: q2(j, lax.rem(j + i, 8)).wait_send())

    def q2_wait(i):
        other = lax.rem(j + i, 8)

        @pl.when(has_span(other, z))
        def _():
            q2(other, j).wait_recv()

    loop(1, 8, q2_wait)

    def w_land(i):
        for h in (0, 1):
            wf(h, i, 0).wait_recv()

    loop(0, NKV, w_land)

    scale = 1.0 / math.sqrt(128)

    def span(n):
        rows = near[n].reshape(256, 896)
        for h in (0, 1):
            keys = jnp.dot(rows, wall[h, 0:896, :], preferred_element_type=F32).astype(BF)
            values = jnp.dot(rows, wall[h, 896:1792, :], preferred_element_type=F32).astype(BF)
            for m in (0, 1):
                cut = slice(128 * m, 128 * m + 128)
                scores = lax.dot_general(q6[n, h, :, cut], keys[:, cut], (((1,), (1,)), ((), ())),
                                         preferred_element_type=F32) * scale
                w = jnp.exp(scores - jnp.max(scores, axis=-1, keepdims=True))
                w = w / jnp.sum(w, axis=-1, keepdims=True)
                o = jnp.dot(w.astype(BF), values[:, cut], preferred_element_type=F32)
                att[j, n, :, 256 * h + 128 * m:256 * h + 128 * m + 128] = o.astype(BF)

    def att_view(block, part):
        return att.at[block, pl.ds(3 * part, 3)]

    def always(block):
        return block >= 0

    for part in (0, 1):
        loop(3 * part, 3 * part + 3, span)
        slots(PACE["span"])
        gather_yc(att_view, here, ts, tr, always, part)
    forward, finish = gather_yc(att_view, here, ts, tr, always, None, lambda: slots(PACE["att_step"]))
    forward()
    slots(LAST)
    finish()
    loop(NKV, NP, w_land)

    def b_copy(g, source, target):
        return remote(res.at[g, slot_of(target, z)], ob.at[g, source], bs.at[g, target], br.at[g, source],
                      dp_of(x, target), z)

    for g in (0, 1):
        acc[...] = jnp.zeros_like(acc)

        def project(b):
            rows = att[b].reshape(384, 512)
            total = acc[...]
            for h in (0, 1):
                first = pl.multiple_of(2048 + (b + 8 * h) * 256, 256)
                total = total + jnp.dot(rows[:, 256 * h:256 * h + 256], wall[g, pl.ds(first, 256), :],
                                        preferred_element_type=F32)
            acc[...] = total

        loop(0, 8, project)
        res[g] = acc[...].astype(BF).reshape(6, 64, 256)

        def b_send(i):
            other = lax.rem(j + i, 8)

            @pl.when(has_span(other, z))
            def _():
                b_copy(g, j, other).start()

        loop(1, 8, b_send)

    def c_local(g, source, k):
        return pltpu.make_async_copy(ob.at[g, source], fb.at[k], lsem.at[0])

    def c_send(g, source):
        to = source + 8 * g
        k = span_of(j, z)

        @pl.when(to == z)
        def _():
            c_local(g, source, k).start()

        @pl.when(to != z)
        def _():
            remote(ob.at[g, source], fb.at[k], cs.at[to], cr.at[k], dp, to).start()

    @pl.when(has_span(j, z))
    def _():
        for g in (0, 1):
            ob[g, j] = res[g, slot_of(j, z)]
            c_send(g, j)

            def relay(i):
                other = lax.rem(j + i, 8)
                b_copy(g, other, j).wait_recv()
                c_send(g, other)

            loop(1, 8, relay)
        c_local(0, 0, 0).wait()

    load_hid.wait()

    def land(k):
        @pl.when(plane_of(j, k) != z)
        def _():
            remote(ob.at[0, 0], fb.at[k], cs.at[0], cr.at[k], dp, z).wait_recv()

        out_ref[k] = (hid_ref[k].astype(F32) + fb[k].astype(F32)).astype(BF)

    loop(0, 12, land)

    def sent(k):
        p, copy = n_copy(k)
        _, copy_q = q_copy(k)

        @pl.when(p != z)
        def _():
            copy.wait_send()
            copy_q.wait_send()

    loop(0, 12, sent)

    def sent_dp(i):
        other = lax.rem(dp + i, 32)
        req_copy(dp, other).wait_send()
        reply(dp, other).wait_send()

    loop(1, 32, sent_dp)

    def sent_w(i):
        wz(s, i, right, 0).wait_send()

        @pl.when(e == 0)
        def _():
            wz(s, i, left, 1).wait_send()

        @pl.when(e >= 2)
        def _():
            wz(1 - s, i, left, 1).wait_send()

        for h in (0, 1):
            wx(h, i, 0).wait_send()
            wx(h, i, 1).wait_send()
            wf(h, i, 0).wait_send()

    loop(0, NP, sent_w)

    def b_sent(i):
        other = lax.rem(j + i, 8)

        @pl.when(has_span(other, z))
        def _():
            b_copy(0, j, other).wait_send()
            b_copy(1, j, other).wait_send()

    loop(1, 8, b_sent)

    @pl.when(has_span(j, z))
    def _():
        def c_sent(i):
            to = lax.rem(z + i, 16)
            remote(ob.at[0, 0], fb.at[0], cs.at[to], cr.at[0], dp, to).wait_send()

        loop(1, 16, c_sent)


def layer(owners, slots, db, queries, w_key, w_value, w_out, hidden):
    dma = pltpu.SemaphoreType.DMA
    any_ = pl.BlockSpec(memory_space=pl.ANY)
    vmem = pl.BlockSpec(memory_space=pltpu.VMEM)
    return pl.pallas_call(
        layer_kernel,
        name="layer",
        out_shape=jax.ShapeDtypeStruct((12, 64, 256), BF),
        in_specs=[vmem, vmem, any_, any_, any_, any_, any_, any_],
        out_specs=vmem,
        scratch_shapes=[
            pltpu.VMEM((256, 896), BF),
            pltpu.VMEM((12, 64, 256), BF),
            pltpu.VMEM((8, 128), jnp.int32),
            pltpu.VMEM((2, 8, 64, 256), BF),
            pltpu.VMEM((6, 2, 64, 256), BF),
            pltpu.VMEM((32, 8, 128), jnp.int32),
            pltpu.VMEM((32, 16, 896), BF),
            pltpu.VMEM((32, 16, 896), BF),
            pltpu.VMEM((12, 16, 896), BF),
            pltpu.VMEM((6, 16, 16, 896), BF),
            pltpu.VMEM((2, NP * 4 * PIECE, 256), BF),
            pltpu.VMEM((8, 6, 64, 512), BF),
            pltpu.VMEM((384, 256), F32),
            pltpu.VMEM((2, 6, 64, 256), BF),
            pltpu.VMEM((2, 8, 64, 256), BF),
            pltpu.VMEM((12, 64, 256), BF),
            dma((32,)), dma((32,)),
            dma((12,)), dma((16,)),
            dma((8,)), dma((8,)),
            dma((32,)), dma((32,)),
            dma((12,)), dma((16,)),
            dma((7, 2)), dma((8, 2)),
            dma((NP,)),
            dma((2, NP)), dma((2, NP)),
            dma((2, 2, NP)), dma((2, 2, NP)),
            dma((2, NP)), dma((2, NP)),
            dma((7, 2)), dma((8, 2)),
            dma((2, 8)), dma((2, 8)),
            dma((16,)), dma((12,)),
            dma((4,)), dma((2,)),
        ],
        compiler_params=pltpu.CompilerParams(
            collective_id=0, has_side_effects=True, vmem_limit_bytes=62 * 2**20
        ),
    )(owners, slots, db, queries, w_key, w_value, w_out, hidden)


def per_device(hidden, queries, database, w_key, w_value, w_out, owners, entry_slots):
    mixed = layer(
        owners.T, entry_slots.T, database.reshape(256, 896), queries.reshape(12, 64, 256),
        w_key, w_value, w_out, hidden.reshape(12, 64, 256),
    )
    return mixed.reshape(768, 256)


def solution(mesh):
    in_specs = (
        P("dp", "tensor"),
        P("dp", "tensor"),
        P("dp", "tensor", None),
        P(None, "tensor"),
        P(None, "tensor"),
        P(None, "tensor"),
        P("dp", None),
        P("dp", None),
    )
    return jax.shard_map(
        per_device, mesh=mesh, in_specs=in_specs, out_specs=P("dp", "tensor"), check_vma=False
    )
```

```python
import functools
import math

import jax
import jax.numpy as jnp
from jax import lax
from jax.experimental import pallas as pl
from jax.experimental.pallas import tpu as pltpu
from jax.sharding import PartitionSpec as P

MESH = pl.DeviceIdType.MESH
BF = jnp.bfloat16
F32 = jnp.float32
NP = 12
NKV = 4
PIECE = 128
SKEW = 1
LAG = 2
LAST = NP + 8 * SKEW + LAG
PACE = dict(ask=2, fetch=4, move=4, near=2, near_step=1, span=1, att_step=1)


def where_am_i():
    dp = lax.axis_index("dp")
    z = lax.axis_index("tensor")
    y = dp // 8
    x = lax.rem(dp // 2, 4)
    c = lax.rem(dp, 2)
    return dp, z, y, x, c, 2 * y + c


def dp_of(x, j):
    return (j // 2) * 8 + x * 2 + lax.rem(j, 2)


def turn(j, p):
    return lax.rem(p // 4 + j, 4)


def has_span(j, p):
    return turn(j, p) < 3


def slot_of(j, p):
    return (j // 4) * 3 + turn(j, p)


def span_of(j, p):
    return 4 * turn(j, p) + lax.rem(p, 4)


def plane_of(j, k):
    return 4 * lax.rem(k // 4 - j + 8, 4) + lax.rem(k, 4)


def remote(src, dst, ssem, rsem, dp, z):
    return pltpu.make_async_remote_copy(
        src_ref=src, dst_ref=dst, send_sem=ssem, recv_sem=rsem,
        device_id=(dp, z), device_id_type=MESH,
    )


def loop(lo, hi, body):
    def step(i, carry):
        body(i)
        return carry

    lax.fori_loop(lo, hi, step, 0)


def gather_yc(view, here, ssem, rsem, good, half, between=None):
    dp, z, y, x, c, j = here

    def at(dy, dc):
        return 2 * lax.rem(y + dy + 4, 4) + lax.rem(c + dc, 2)

    def send(block, part, target, number):
        return remote(view(block, part), view(block, part), ssem.at[number, part],
                      rsem.at[block, part], dp_of(x, target), z)

    up, down, twin, far = at(1, 0), at(-1, 0), at(0, 1), at(2, 0)
    if half is not None:

        @pl.when(good(j))
        def _():
            send(j, half, up, 0).start()
            send(j, half, down, 1).start()
            send(j, half, twin, 2).start()

        return None

    def forward():
        for part in (0, 1):

            @pl.when(good(down))
            def _():
                send(down, part, j, 0).wait_recv()
                if part == 0:
                    send(down, part, up, 6).start()
                send(down, part, twin, 3).start()

            @pl.when(good(up))
            def _():
                send(up, part, j, 0).wait_recv()
                if part == 1:
                    send(up, part, down, 6).start()
                send(up, part, twin, 4).start()

            between()

        for part in (0, 1):

            @pl.when(good(far))
            def _():
                send(far, part, j, 0).wait_recv()
                send(far, part, twin, 5).start()

            between()

    def finish():
        for part in (0, 1):
            for dy in (0, 1, 3, 2):
                other = at(dy, 1)

                @pl.when(good(other))
                def _():
                    send(other, part, j, 0).wait_recv()

            @pl.when(good(j))
            def _():
                for number in (0, 1, 2):
                    send(j, part, twin, number).wait_send()

            for number, block in ((3, down), (4, up), (5, far)):

                @pl.when(good(block))
                def _():
                    send(block, part, twin, number).wait_send()

        @pl.when(good(down))
        def _():
            send(down, 0, up, 6).wait_send()

        @pl.when(good(up))
        def _():
            send(up, 1, down, 6).wait_send()

    return forward, finish


def layer_kernel(own_ref, ent_ref, db_hbm, q_ref, wk_ref, wv_ref, wo_ref, hid_hbm, out_ref,
                 db_ref, hid_ref, req_ref, qa, q6, rall, served, replies, mine, near, wall, att, res, ob, fb,
                 rs, rr, qs, qr, q2s, q2r, as_, ar, ns, nr, gs, gr,
                 wl, zs, zr, xs, xr, fs, fr, ts, tr, bs, br, cs, cr, lsem, load):
    here = where_am_i()
    dp, z, y, x, c, j = here
    d = lax.rem(z - j + 16, 16)
    e, s = lax.rem(d, 8), d // 8
    right, left = lax.rem(z + 1, 16), lax.rem(z + 15, 16)
    xright, xleft = lax.rem(x + 1, 4), lax.rem(x + 3, 4)

    def piece(h, i, chunk):
        return wall.at[h, pl.ds(pl.multiple_of((4 * i + chunk) * PIECE, PIECE), PIECE)]

    load_db = pltpu.make_async_copy(db_hbm, db_ref, load.at[0])
    load_hid = pltpu.make_async_copy(hid_hbm, hid_ref, load.at[1])
    load_db.start()

    def own_rows(ref, g):
        return ref.at[pl.ds(pl.multiple_of(g * PIECE, PIECE), PIECE)]

    def own(i, ref, g):
        return pltpu.make_async_copy(own_rows(ref, g), piece(s, i, x), wl.at[i])

    @pl.when(e == 0)
    def _():
        for i in range(NKV):
            g = 4 * i + x

            @pl.when(g < 7)
            def _():
                own(i, wk_ref, jnp.minimum(g, 6)).start()

            @pl.when(g >= 7)
            def _():
                own(i, wv_ref, jnp.clip(g - 7, 0, 6)).start()

        for i in range(NKV, NP):
            own(i, wo_ref, 2 * (i - NKV) + 16 * (x // 2) + lax.rem(x, 2)).start()

    load_hid.start()
    barrier = pltpu.get_barrier_semaphore()

    def greet(i):
        pl.semaphore_signal(barrier, inc=1, device_id=(lax.rem(dp + i, 32), z), device_id_type=MESH)

    def greet_z(i):
        pl.semaphore_signal(barrier, inc=1, device_id=(dp, lax.rem(z + i, 16)), device_id_type=MESH)

    loop(1, 32, greet)
    loop(1, 16, greet_z)
    pl.semaphore_wait(barrier, 46)

    number = lax.broadcasted_iota(jnp.int32, (24, 12), 0)
    lane = lax.broadcasted_iota(jnp.int32, (24, 12), 1)

    def column(ref):
        both = jnp.where(number < 12, ref[0:1, :], ref[1:2, :])
        return jnp.sum(jnp.where(lane == number % 12, both, 0), axis=1, keepdims=True)

    wanted = column(own_ref)
    order = jnp.zeros((24, 1), jnp.int32)
    for n in (0, 1):
        earlier = (own_ref[n:n + 1, :] == wanted) & (lane + 12 * n < number)
        order = order + jnp.sum(earlier.astype(jnp.int32), axis=1, keepdims=True)
    placed = (2 * wanted + order) == lax.broadcasted_iota(jnp.int32, (24, 128), 1)
    row = jnp.sum(jnp.where(placed, column(ent_ref) + 1, 0), axis=0, keepdims=True)
    req_ref[...] = jnp.broadcast_to(row, (8, 128))

    def req_copy(source, target):
        return remote(req_ref, rall.at[source], rs.at[target], rr.at[source], target, z)

    loop(1, 32, lambda i: req_copy(dp, lax.rem(dp + i, 32)).start())

    def wz(h, i, to, way):
        return remote(piece(h, i, x), piece(h, i, x), zs.at[way, i], zr.at[h, i], dp, to)

    def wx(h, i, way):
        return remote(piece(h, i, x), piece(h, i, x), xs.at[way, h, i], xr.at[way, h, i],
                      dp_of(xright if way == 0 else xleft, j), z)

    def wx_in(h, i, way):
        chunk = xleft if way == 0 else xright
        return remote(piece(h, i, chunk), piece(h, i, chunk), fs.at[h, i], xr.at[way, h, i],
                      dp_of(xright, j), z)

    def wf(h, i, way):
        chunk = xleft if way == 0 else xright
        return remote(piece(h, i, chunk), piece(h, i, chunk), fs.at[h, i], fr.at[h, i],
                      dp_of(xright if way == 0 else xleft, j), z)

    def inject(lo, hi):
        @pl.when(e == 0)
        def _():
            def one(i):
                own(i, wo_ref, 0).wait()
                wz(s, i, right, 0).start()
                wz(s, i, left, 1).start()

            loop(lo, hi, one)

    inject(0, NP)

    def q_copy(k):
        p = plane_of(j, k)
        return p, remote(q_ref.at[k], qa.at[z // 8, lax.rem(z, 8)], qs.at[k],
                         qr.at[z], dp, p)

    def q_local(k):
        return pltpu.make_async_copy(q_ref.at[k], qa.at[z // 8, lax.rem(z, 8)], lsem.at[1])

    def q_send(k):
        p, copy = q_copy(k)

        @pl.when(p == z)
        def _():
            q_local(k).start()

        @pl.when(p != z)
        def _():
            copy.start()

    loop(0, 12, q_send)

    def slot(t):
        ia = t - SKEW * e
        ib = t - SKEW * (8 - e)

        @pl.when((ia >= 0) & (ia < NP))
        def _():
            @pl.when(e > 0)
            def _():
                wz(s, ia, z, 0).wait_recv()
                wz(s, ia, right, 0).start()

            wx(s, ia, 0).start()
            wx(s, ia, 1).start()

        @pl.when((ib >= 0) & (ib < NP))
        def _():
            wz(1 - s, ib, z, 0).wait_recv()

            @pl.when(e >= 2)
            def _():
                wz(1 - s, ib, left, 1).start()

            wx(1 - s, ib, 0).start()
            wx(1 - s, ib, 1).start()

        for h, i in ((s, ia - LAG), (1 - s, ib - LAG)):

            @pl.when((i >= 0) & (i < NP))
            def _():
                wx_in(h, i, 0).wait_recv()
                wx_in(h, i, 1).wait_recv()

                @pl.when(lax.rem(i, 2) == 0)
                def _():
                    wf(h, i, 0).start()

                @pl.when(lax.rem(i, 2) == 1)
                def _():
                    wf(h, i, 1).start()

    done = [0]

    def slots(count):
        upto = min(done[0] + count, LAST)
        if upto > done[0]:
            loop(done[0], upto, slot)
        done[0] = upto

    slots(PACE["ask"])

    rall[dp] = req_ref[...]
    loop(1, 32, lambda i: req_copy(lax.rem(dp + i, 32), dp).wait_recv())
    load_db.wait()
    table = rall[:, 0, :].astype(F32).astype(BF)
    expand = (lax.broadcasted_iota(jnp.int32, (512, 32), 0) // 16
              == lax.broadcasted_iota(jnp.int32, (512, 32), 1)).astype(F32).astype(BF)
    spread = jnp.dot(expand, table, preferred_element_type=F32)
    row = lax.broadcasted_iota(jnp.int32, (512, 128), 0)
    lane = lax.broadcasted_iota(jnp.int32, (512, 128), 1)
    entry = jnp.sum(jnp.where(lane == 2 * dp + (row // 8) % 2, spread, 0.0), axis=1, keepdims=True)
    row = lax.broadcasted_iota(jnp.int32, (512, 256), 0)
    column = lax.broadcasted_iota(jnp.int32, (512, 256), 1)
    hot = ((column // 8 + 1).astype(F32) == entry) & (column % 8 == row % 8)
    picked = jnp.dot(hot.astype(F32).astype(BF), db_ref[...], preferred_element_type=F32)
    served[...] = picked.astype(BF).reshape(32, 16, 896)

    def reply(source, target):
        return remote(served.at[target], replies.at[source], as_.at[target], ar.at[source], target, z)

    loop(1, 32, lambda i: reply(dp, lax.rem(dp + i, 32)).start())
    r = lax.broadcasted_iota(jnp.int32, (192, 24), 0)
    request = lax.broadcasted_iota(jnp.int32, (192, 24), 1) == 12 * ((r // 8) % 2) + r // 16
    spread = jnp.dot(request.astype(F32).astype(BF), placed.astype(F32).astype(BF), preferred_element_type=F32)
    widen = (lax.broadcasted_iota(jnp.int32, (128, 512), 1) // 8
             == lax.broadcasted_iota(jnp.int32, (128, 512), 0))
    spread = jnp.dot(spread.astype(BF), widen.astype(F32).astype(BF), preferred_element_type=F32)
    token = (lax.broadcasted_iota(jnp.int32, (192, 512), 0) % 8
             == lax.broadcasted_iota(jnp.int32, (192, 512), 1) % 8)
    sel = jnp.where(token, spread, 0.0).astype(BF)
    slots(PACE["fetch"])
    replies[dp] = served[dp]
    loop(1, 32, lambda i: reply(lax.rem(dp + i, 32), dp).wait_recv())
    got = jnp.dot(sel, replies[...].reshape(512, 896), preferred_element_type=F32)
    mine[...] = got.astype(BF).reshape(12, 16, 896)

    def n_copy(k):
        p = plane_of(j, k)
        return p, remote(mine.at[k], near.at[slot_of(j, p), z], ns.at[k], nr.at[z], dp, p)

    def n_local(k):
        return pltpu.make_async_copy(mine.at[k], near.at[slot_of(j, z), z], lsem.at[2])

    def n_send(k):
        p, copy = n_copy(k)

        @pl.when(p == z)
        def _():
            n_local(k).start()

        @pl.when(p != z)
        def _():
            copy.start()

    loop(0, 12, n_send)
    slots(PACE["move"])

    def q2(source, target):
        return remote(qa.at[:, target], q6.at[slot_of(source, z)], q2s.at[target], q2r.at[source],
                      dp_of(x, target), z)

    def q2_local():
        return pltpu.make_async_copy(qa.at[:, j], q6.at[slot_of(j, z)], lsem.at[3])

    @pl.when(has_span(j, z))
    def _():
        q_local(0).wait()
        loop(1, 16, lambda i: remote(q_ref.at[0], qa.at[0, 0], qs.at[0], qr.at[lax.rem(z + i, 16)],
                                     dp, z).wait_recv())
        q2_local().start()
        loop(1, 8, lambda i: q2(j, lax.rem(j + i, 8)).start())


    def view(block, part):
        return near.at[slot_of(block, z), pl.ds(part * 8, 8)]

    def good(block):
        return has_span(block, z)

    @pl.when(good(j))
    def _():
        n_local(0).wait()
        loop(1, 16, lambda i: remote(mine.at[0], near.at[0, 0], ns.at[0], nr.at[lax.rem(z + i, 16)],
                                     dp, z).wait_recv())

    for part in (0, 1):
        gather_yc(view, here, gs, gr, good, part)
    slots(PACE["near"])
    forward, finish = gather_yc(view, here, gs, gr, good, None, lambda: slots(PACE["near_step"]))
    forward()
    finish()

    @pl.when(has_span(j, z))
    def _():
        q2_local().wait()
        loop(1, 8, lambda i: q2(j, lax.rem(j + i, 8)).wait_send())

    def q2_wait(i):
        other = lax.rem(j + i, 8)

        @pl.when(has_span(other, z))
        def _():
            q2(other, j).wait_recv()

    loop(1, 8, q2_wait)

    def w_land(i):
        for h in (0, 1):
            wf(h, i, 0).wait_recv()

    loop(0, NKV, w_land)

    scale = 1.0 / math.sqrt(128)

    def span(n):
        rows = near[n].reshape(256, 896)
        for h in (0, 1):
            keys = jnp.dot(rows, wall[h, 0:896, :], preferred_element_type=F32).astype(BF)
            values = jnp.dot(rows, wall[h, 896:1792, :], preferred_element_type=F32).astype(BF)
            for m in (0, 1):
                cut = slice(128 * m, 128 * m + 128)
                scores = lax.dot_general(q6[n, h, :, cut], keys[:, cut], (((1,), (1,)), ((), ())),
                                         preferred_element_type=F32) * scale
                w = jnp.exp(scores - jnp.max(scores, axis=-1, keepdims=True))
                w = w / jnp.sum(w, axis=-1, keepdims=True)
                o = jnp.dot(w.astype(BF), values[:, cut], preferred_element_type=F32)
                att[j, n, :, 256 * h + 128 * m:256 * h + 128 * m + 128] = o.astype(BF)

    def att_view(block, part):
        return att.at[block, pl.ds(3 * part, 3)]

    def always(block):
        return block >= 0

    for part in (0, 1):
        loop(3 * part, 3 * part + 3, span)
        slots(PACE["span"])
        gather_yc(att_view, here, ts, tr, always, part)
    forward, finish = gather_yc(att_view, here, ts, tr, always, None, lambda: slots(PACE["att_step"]))
    forward()
    slots(LAST)
    finish()
    loop(NKV, NP, w_land)

    def b_copy(g, source, target):
        return remote(res.at[g, slot_of(target, z)], ob.at[g, source], bs.at[g, target], br.at[g, source],
                      dp_of(x, target), z)

    for g in (0, 1):
        def project(n):
            total = None
            for b in range(8):
                rows = att[b, pl.ds(3 * n, 3)].reshape(192, 512)
                part = jnp.dot(rows, wall[g, 2048 + 512 * b:2560 + 512 * b, :], preferred_element_type=F32)
                total = part if total is None else total + part
            res[g, pl.ds(3 * n, 3)] = total.astype(BF).reshape(3, 64, 256)

        loop(0, 2, project)

        def b_send(i):
            other = lax.rem(j + i, 8)

            @pl.when(has_span(other, z))
            def _():
                b_copy(g, j, other).start()

        loop(1, 8, b_send)

    def c_local(g, source, k):
        return pltpu.make_async_copy(ob.at[g, source], fb.at[k], lsem.at[0])

    def c_send(g, source):
        to = source + 8 * g
        k = span_of(j, z)

        @pl.when(to == z)
        def _():
            c_local(g, source, k).start()

        @pl.when(to != z)
        def _():
            remote(ob.at[g, source], fb.at[k], cs.at[to], cr.at[k], dp, to).start()

    @pl.when(has_span(j, z))
    def _():
        for g in (0, 1):
            ob[g, j] = res[g, slot_of(j, z)]
            c_send(g, j)

            def relay(i):
                other = lax.rem(j + i, 8)
                b_copy(g, other, j).wait_recv()
                c_send(g, other)

            loop(1, 8, relay)
        c_local(0, 0, 0).wait()

    load_hid.wait()

    def land(k):
        @pl.when(plane_of(j, k) != z)
        def _():
            remote(ob.at[0, 0], fb.at[k], cs.at[0], cr.at[k], dp, z).wait_recv()

        out_ref[k] = (hid_ref[k].astype(F32) + fb[k].astype(F32)).astype(BF)

    loop(0, 12, land)

    def sent(k):
        p, copy = n_copy(k)
        _, copy_q = q_copy(k)

        @pl.when(p != z)
        def _():
            copy.wait_send()
            copy_q.wait_send()

    loop(0, 12, sent)

    def sent_dp(i):
        other = lax.rem(dp + i, 32)
        req_copy(dp, other).wait_send()
        reply(dp, other).wait_send()

    loop(1, 32, sent_dp)

    def sent_w(i):
        wz(s, i, right, 0).wait_send()

        @pl.when(e == 0)
        def _():
            wz(s, i, left, 1).wait_send()

        @pl.when(e >= 2)
        def _():
            wz(1 - s, i, left, 1).wait_send()

        for h in (0, 1):
            wx(h, i, 0).wait_send()
            wx(h, i, 1).wait_send()
            wf(h, i, 0).wait_send()

    loop(0, NP, sent_w)

    def b_sent(i):
        other = lax.rem(j + i, 8)

        @pl.when(has_span(other, z))
        def _():
            b_copy(0, j, other).wait_send()
            b_copy(1, j, other).wait_send()

    loop(1, 8, b_sent)

    @pl.when(has_span(j, z))
    def _():
        def c_sent(i):
            to = lax.rem(z + i, 16)
            remote(ob.at[0, 0], fb.at[0], cs.at[to], cr.at[0], dp, to).wait_send()

        loop(1, 16, c_sent)


def layer(owners, slots, db, queries, w_key, w_value, w_out, hidden):
    dma = pltpu.SemaphoreType.DMA
    any_ = pl.BlockSpec(memory_space=pl.ANY)
    vmem = pl.BlockSpec(memory_space=pltpu.VMEM)
    return pl.pallas_call(
        layer_kernel,
        name="layer",
        out_shape=jax.ShapeDtypeStruct((12, 64, 256), BF),
        in_specs=[vmem, vmem, any_, any_, any_, any_, any_, any_],
        out_specs=vmem,
        scratch_shapes=[
            pltpu.VMEM((256, 896), BF),
            pltpu.VMEM((12, 64, 256), BF),
            pltpu.VMEM((8, 128), jnp.int32),
            pltpu.VMEM((2, 8, 64, 256), BF),
            pltpu.VMEM((6, 2, 64, 256), BF),
            pltpu.VMEM((32, 8, 128), jnp.int32),
            pltpu.VMEM((32, 16, 896), BF),
            pltpu.VMEM((32, 16, 896), BF),
            pltpu.VMEM((12, 16, 896), BF),
            pltpu.VMEM((6, 16, 16, 896), BF),
            pltpu.VMEM((2, NP * 4 * PIECE, 256), BF),
            pltpu.VMEM((8, 6, 64, 512), BF),
            pltpu.VMEM((2, 6, 64, 256), BF),
            pltpu.VMEM((2, 8, 64, 256), BF),
            pltpu.VMEM((12, 64, 256), BF),
            dma((32,)), dma((32,)),
            dma((12,)), dma((16,)),
            dma((8,)), dma((8,)),
            dma((32,)), dma((32,)),
            dma((12,)), dma((16,)),
            dma((7, 2)), dma((8, 2)),
            dma((NP,)),
            dma((2, NP)), dma((2, NP)),
            dma((2, 2, NP)), dma((2, 2, NP)),
            dma((2, NP)), dma((2, NP)),
            dma((7, 2)), dma((8, 2)),
            dma((2, 8)), dma((2, 8)),
            dma((16,)), dma((12,)),
            dma((4,)), dma((2,)),
        ],
        compiler_params=pltpu.CompilerParams(
            collective_id=0, has_side_effects=True, vmem_limit_bytes=62 * 2**20
        ),
    )(owners, slots, db, queries, w_key, w_value, w_out, hidden)


def per_device(hidden, queries, database, w_key, w_value, w_out, owners, entry_slots):
    mixed = layer(
        owners.T, entry_slots.T, database.reshape(256, 896), queries.reshape(12, 64, 256),
        w_key, w_value, w_out, hidden.reshape(12, 64, 256),
    )
    return mixed.reshape(768, 256)


def solution(mesh):
    in_specs = (
        P("dp", "tensor"),
        P("dp", "tensor"),
        P("dp", "tensor", None),
        P(None, "tensor"),
        P(None, "tensor"),
        P(None, "tensor"),
        P("dp", None),
        P("dp", None),
    )
    return jax.shard_map(
        per_device, mesh=mesh, in_specs=in_specs, out_specs=P("dp", "tensor"), check_vma=False
    )
```

```python
import functools
import math

import jax
import jax.numpy as jnp
from jax import lax
from jax.experimental import pallas as pl
from jax.experimental.pallas import tpu as pltpu
from jax.sharding import PartitionSpec as P

MESH = pl.DeviceIdType.MESH
BF = jnp.bfloat16
F32 = jnp.float32
NP = 12
NKV = 4
PIECE = 128
SKEW = 1
LAG = 2
LAST = NP + 8 * SKEW + LAG
PACE = dict(ask=2, fetch=4, move=4, near=2, near_step=1, span=1, att_step=1)


def where_am_i():
    dp = lax.axis_index("dp")
    z = lax.axis_index("tensor")
    y = dp // 8
    x = lax.rem(dp // 2, 4)
    c = lax.rem(dp, 2)
    return dp, z, y, x, c, 2 * y + c


def dp_of(x, j):
    return (j // 2) * 8 + x * 2 + lax.rem(j, 2)


def turn(j, p):
    return lax.rem(p // 4 + j, 4)


def has_span(j, p):
    return turn(j, p) < 3


def slot_of(j, p):
    return (j // 4) * 3 + turn(j, p)


def span_of(j, p):
    return 4 * turn(j, p) + lax.rem(p, 4)


def plane_of(j, k):
    return 4 * lax.rem(k // 4 - j + 8, 4) + lax.rem(k, 4)


def remote(src, dst, ssem, rsem, dp, z):
    return pltpu.make_async_remote_copy(
        src_ref=src, dst_ref=dst, send_sem=ssem, recv_sem=rsem,
        device_id=(dp, z), device_id_type=MESH,
    )


def loop(lo, hi, body):
    def step(i, carry):
        body(i)
        return carry

    lax.fori_loop(lo, hi, step, 0)


def gather_yc(view, here, ssem, rsem, good, half, between=None):
    dp, z, y, x, c, j = here

    def at(dy, dc):
        return 2 * lax.rem(y + dy + 4, 4) + lax.rem(c + dc, 2)

    def send(block, part, target, number):
        return remote(view(block, part), view(block, part), ssem.at[number, part],
                      rsem.at[block, part], dp_of(x, target), z)

    up, down, twin, far = at(1, 0), at(-1, 0), at(0, 1), at(2, 0)
    if half is not None:

        @pl.when(good(j))
        def _():
            send(j, half, up, 0).start()
            send(j, half, down, 1).start()
            send(j, half, twin, 2).start()

        return None

    def forward():
        for part in (0, 1):

            @pl.when(good(down))
            def _():
                send(down, part, j, 0).wait_recv()
                if part == 0:
                    send(down, part, up, 6).start()
                send(down, part, twin, 3).start()

            @pl.when(good(up))
            def _():
                send(up, part, j, 0).wait_recv()
                if part == 1:
                    send(up, part, down, 6).start()
                send(up, part, twin, 4).start()

            between()

        for part in (0, 1):

            @pl.when(good(far))
            def _():
                send(far, part, j, 0).wait_recv()
                send(far, part, twin, 5).start()

            between()

    def finish():
        for part in (0, 1):
            for dy in (0, 1, 3, 2):
                other = at(dy, 1)

                @pl.when(good(other))
                def _():
                    send(other, part, j, 0).wait_recv()

            @pl.when(good(j))
            def _():
                for number in (0, 1, 2):
                    send(j, part, twin, number).wait_send()

            for number, block in ((3, down), (4, up), (5, far)):

                @pl.when(good(block))
                def _():
                    send(block, part, twin, number).wait_send()

        @pl.when(good(down))
        def _():
            send(down, 0, up, 6).wait_send()

        @pl.when(good(up))
        def _():
            send(up, 1, down, 6).wait_send()

    return forward, finish


def layer_kernel(own_ref, ent_ref, db_hbm, q_ref, wk_ref, wv_ref, wo_ref, hid_hbm, out_ref,
                 db_ref, hid_ref, req_ref, qa, q6, rall, served, replies, mine, near, wall, att, res, ob, fb,
                 rs, rr, qs, qr, q2s, q2r, as_, ar, ns, nr, gs, gr,
                 wl, zs, zr, xs, xr, fs, fr, ts, tr, bs, br, cs, cr, lsem, load):
    here = where_am_i()
    dp, z, y, x, c, j = here
    d = lax.rem(z - j + 16, 16)
    e, s = lax.rem(d, 8), d // 8
    right, left = lax.rem(z + 1, 16), lax.rem(z + 15, 16)
    xright, xleft = lax.rem(x + 1, 4), lax.rem(x + 3, 4)

    def piece(h, i, chunk):
        return wall.at[h, pl.ds(pl.multiple_of((4 * i + chunk) * PIECE, PIECE), PIECE)]

    load_db = pltpu.make_async_copy(db_hbm, db_ref, load.at[0])
    load_hid = pltpu.make_async_copy(hid_hbm, hid_ref, load.at[1])
    load_db.start()

    def own_rows(ref, g):
        return ref.at[pl.ds(pl.multiple_of(g * PIECE, PIECE), PIECE)]

    def own(i, ref, g):
        return pltpu.make_async_copy(own_rows(ref, g), piece(s, i, x), wl.at[i])

    @pl.when(e == 0)
    def _():
        for i in range(NKV):
            g = 4 * i + x

            @pl.when(g < 7)
            def _():
                own(i, wk_ref, jnp.minimum(g, 6)).start()

            @pl.when(g >= 7)
            def _():
                own(i, wv_ref, jnp.clip(g - 7, 0, 6)).start()

        for i in range(NKV, NP):
            own(i, wo_ref, 2 * (i - NKV) + 16 * (x // 2) + lax.rem(x, 2)).start()

    load_hid.start()
    barrier = pltpu.get_barrier_semaphore()

    def greet(i):
        pl.semaphore_signal(barrier, inc=1, device_id=(lax.rem(dp + i, 32), z), device_id_type=MESH)

    def greet_z(i):
        pl.semaphore_signal(barrier, inc=1, device_id=(dp, lax.rem(z + i, 16)), device_id_type=MESH)

    loop(1, 32, greet)
    loop(1, 16, greet_z)
    pl.semaphore_wait(barrier, 46)

    number = lax.broadcasted_iota(jnp.int32, (24, 12), 0)
    lane = lax.broadcasted_iota(jnp.int32, (24, 12), 1)

    def column(ref):
        both = jnp.where(number < 12, ref[0:1, :], ref[1:2, :])
        return jnp.sum(jnp.where(lane == number % 12, both, 0), axis=1, keepdims=True)

    wanted = column(own_ref)
    order = jnp.zeros((24, 1), jnp.int32)
    for n in (0, 1):
        earlier = (own_ref[n:n + 1, :] == wanted) & (lane + 12 * n < number)
        order = order + jnp.sum(earlier.astype(jnp.int32), axis=1, keepdims=True)
    placed = (2 * wanted + order) == lax.broadcasted_iota(jnp.int32, (24, 128), 1)
    row = jnp.sum(jnp.where(placed, column(ent_ref) + 1, 0), axis=0, keepdims=True)
    req_ref[...] = jnp.broadcast_to(row, (8, 128))

    def req_copy(source, target):
        return remote(req_ref, rall.at[source], rs.at[target], rr.at[source], target, z)

    loop(1, 32, lambda i: req_copy(dp, lax.rem(dp + i, 32)).start())

    def wz(h, i, to, way):
        return remote(piece(h, i, x), piece(h, i, x), zs.at[way, i], zr.at[h, i], dp, to)

    def wx(h, i, way):
        return remote(piece(h, i, x), piece(h, i, x), xs.at[way, h, i], xr.at[way, h, i],
                      dp_of(xright if way == 0 else xleft, j), z)

    def wx_in(h, i, way):
        chunk = xleft if way == 0 else xright
        return remote(piece(h, i, chunk), piece(h, i, chunk), fs.at[h, i], xr.at[way, h, i],
                      dp_of(xright, j), z)

    def wf(h, i, way):
        chunk = xleft if way == 0 else xright
        return remote(piece(h, i, chunk), piece(h, i, chunk), fs.at[h, i], fr.at[h, i],
                      dp_of(xright if way == 0 else xleft, j), z)

    def inject(lo, hi):
        @pl.when(e == 0)
        def _():
            def one(i):
                own(i, wo_ref, 0).wait()
                wz(s, i, right, 0).start()
                wz(s, i, left, 1).start()

            loop(lo, hi, one)

    inject(0, NP)

    def q_copy(k):
        p = plane_of(j, k)
        return p, remote(q_ref.at[k], qa.at[z // 8, lax.rem(z, 8)], qs.at[k],
                         qr.at[z], dp, p)

    def q_local(k):
        return pltpu.make_async_copy(q_ref.at[k], qa.at[z // 8, lax.rem(z, 8)], lsem.at[1])

    def q_send(k):
        p, copy = q_copy(k)

        @pl.when(p == z)
        def _():
            q_local(k).start()

        @pl.when(p != z)
        def _():
            copy.start()

    loop(0, 12, q_send)

    def slot(t):
        ia = t - SKEW * e
        ib = t - SKEW * (8 - e)

        @pl.when((ia >= 0) & (ia < NP))
        def _():
            @pl.when(e > 0)
            def _():
                wz(s, ia, z, 0).wait_recv()
                wz(s, ia, right, 0).start()

            wx(s, ia, 0).start()
            wx(s, ia, 1).start()

        @pl.when((ib >= 0) & (ib < NP))
        def _():
            wz(1 - s, ib, z, 0).wait_recv()

            @pl.when(e >= 2)
            def _():
                wz(1 - s, ib, left, 1).start()

            wx(1 - s, ib, 0).start()
            wx(1 - s, ib, 1).start()

        for h, i in ((s, ia - LAG), (1 - s, ib - LAG)):

            @pl.when((i >= 0) & (i < NP))
            def _():
                wx_in(h, i, 0).wait_recv()
                wx_in(h, i, 1).wait_recv()

                @pl.when(lax.rem(i, 2) == 0)
                def _():
                    wf(h, i, 0).start()

                @pl.when(lax.rem(i, 2) == 1)
                def _():
                    wf(h, i, 1).start()

    done = [0]

    def slots(count):
        upto = min(done[0] + count, LAST)
        if upto > done[0]:
            loop(done[0], upto, slot)
        done[0] = upto

    slots(PACE["ask"])

    rall[dp] = req_ref[...]
    loop(1, 32, lambda i: req_copy(lax.rem(dp + i, 32), dp).wait_recv())
    load_db.wait()
    table = rall[:, 0, :].astype(F32).astype(BF)
    expand = (lax.broadcasted_iota(jnp.int32, (512, 32), 0) // 16
              == lax.broadcasted_iota(jnp.int32, (512, 32), 1)).astype(F32).astype(BF)
    spread = jnp.dot(expand, table, preferred_element_type=F32)
    row = lax.broadcasted_iota(jnp.int32, (512, 128), 0)
    lane = lax.broadcasted_iota(jnp.int32, (512, 128), 1)
    entry = jnp.sum(jnp.where(lane == 2 * dp + (row // 8) % 2, spread, 0.0), axis=1, keepdims=True)
    row = lax.broadcasted_iota(jnp.int32, (512, 256), 0)
    column = lax.broadcasted_iota(jnp.int32, (512, 256), 1)
    hot = ((column // 8 + 1).astype(F32) == entry) & (column % 8 == row % 8)
    picked = jnp.dot(hot.astype(F32).astype(BF), db_ref[...], preferred_element_type=F32)
    served[...] = picked.astype(BF).reshape(32, 16, 896)

    def reply(source, target):
        return remote(served.at[target], replies.at[source], as_.at[target], ar.at[source], target, z)

    loop(1, 32, lambda i: reply(dp, lax.rem(dp + i, 32)).start())
    r = lax.broadcasted_iota(jnp.int32, (192, 24), 0)
    request = lax.broadcasted_iota(jnp.int32, (192, 24), 1) == 12 * ((r // 8) % 2) + r // 16
    spread = jnp.dot(request.astype(F32).astype(BF), placed.astype(F32).astype(BF), preferred_element_type=F32)
    widen = (lax.broadcasted_iota(jnp.int32, (128, 512), 1) // 8
             == lax.broadcasted_iota(jnp.int32, (128, 512), 0))
    spread = jnp.dot(spread.astype(BF), widen.astype(F32).astype(BF), preferred_element_type=F32)
    token = (lax.broadcasted_iota(jnp.int32, (192, 512), 0) % 8
             == lax.broadcasted_iota(jnp.int32, (192, 512), 1) % 8)
    sel = jnp.where(token, spread, 0.0).astype(BF)
    slots(PACE["fetch"])
    replies[dp] = served[dp]
    loop(1, 32, lambda i: reply(lax.rem(dp + i, 32), dp).wait_recv())
    got = jnp.dot(sel, replies[...].reshape(512, 896), preferred_element_type=F32)
    mine[...] = got.astype(BF).reshape(12, 16, 896)

    def n_copy(k):
        p = plane_of(j, k)
        return p, remote(mine.at[k], near.at[slot_of(j, p), z], ns.at[k], nr.at[z], dp, p)

    def n_local(k):
        return pltpu.make_async_copy(mine.at[k], near.at[slot_of(j, z), z], lsem.at[2])

    def n_send(k):
        p, copy = n_copy(k)

        @pl.when(p == z)
        def _():
            n_local(k).start()

        @pl.when(p != z)
        def _():
            copy.start()

    loop(0, 12, n_send)
    slots(PACE["move"])

    def q2(source, target):
        return remote(qa.at[:, target], q6.at[slot_of(source, z)], q2s.at[target], q2r.at[source],
                      dp_of(x, target), z)

    def q2_local():
        return pltpu.make_async_copy(qa.at[:, j], q6.at[slot_of(j, z)], lsem.at[3])

    @pl.when(has_span(j, z))
    def _():
        q_local(0).wait()
        loop(1, 16, lambda i: remote(q_ref.at[0], qa.at[0, 0], qs.at[0], qr.at[lax.rem(z + i, 16)],
                                     dp, z).wait_recv())
        q2_local().start()
        loop(1, 8, lambda i: q2(j, lax.rem(j + i, 8)).start())


    def view(block, part):
        return near.at[slot_of(block, z), pl.ds(8 * lax.rem(part + z // 8, 2), 8)]

    def good(block):
        return has_span(block, z)

    def n_land(source):
        remote(mine.at[0], near.at[0, 0], ns.at[0], nr.at[source], dp, z).wait_recv()

    for part in (0, 1):
        @pl.when(good(j))
        def _():
            half = 8 * lax.rem(part + z // 8, 2)
            if part == 0:
                n_local(0).wait()
            loop(1 - part, 8, lambda i: n_land(half + lax.rem(z + i, 8)))

        gather_yc(view, here, gs, gr, good, part)
    slots(PACE["near"])
    forward, finish = gather_yc(view, here, gs, gr, good, None, lambda: slots(PACE["near_step"]))
    forward()
    finish()

    @pl.when(has_span(j, z))
    def _():
        q2_local().wait()
        loop(1, 8, lambda i: q2(j, lax.rem(j + i, 8)).wait_send())

    def q2_wait(i):
        other = lax.rem(j + i, 8)

        @pl.when(has_span(other, z))
        def _():
            q2(other, j).wait_recv()

    loop(1, 8, q2_wait)

    def w_land(i):
        for h in (0, 1):
            wf(h, i, 0).wait_recv()

    loop(0, NKV, w_land)

    scale = 1.0 / math.sqrt(128)

    def span(n):
        rows = near[n].reshape(256, 896)
        for h in (0, 1):
            keys = jnp.dot(rows, wall[h, 0:896, :], preferred_element_type=F32).astype(BF)
            values = jnp.dot(rows, wall[h, 896:1792, :], preferred_element_type=F32).astype(BF)
            for m in (0, 1):
                cut = slice(128 * m, 128 * m + 128)
                scores = lax.dot_general(q6[n, h, :, cut], keys[:, cut], (((1,), (1,)), ((), ())),
                                         preferred_element_type=F32) * scale
                w = jnp.exp(scores - jnp.max(scores, axis=-1, keepdims=True))
                w = w / jnp.sum(w, axis=-1, keepdims=True)
                o = jnp.dot(w.astype(BF), values[:, cut], preferred_element_type=F32)
                att[j, n, :, 256 * h + 128 * m:256 * h + 128 * m + 128] = o.astype(BF)

    def att_view(block, part):
        return att.at[block, pl.ds(3 * part, 3)]

    def always(block):
        return block >= 0

    for part in (0, 1):
        loop(3 * part, 3 * part + 3, span)
        slots(PACE["span"])
        gather_yc(att_view, here, ts, tr, always, part)
    forward, finish = gather_yc(att_view, here, ts, tr, always, None, lambda: slots(PACE["att_step"]))
    forward()
    slots(LAST)
    finish()
    loop(NKV, NP, w_land)

    def b_copy(g, source, target):
        return remote(res.at[g, slot_of(target, z)], ob.at[g, source], bs.at[g, target], br.at[g, source],
                      dp_of(x, target), z)

    for g in (0, 1):
        def project(n):
            total = None
            for b in range(8):
                rows = att[b, pl.ds(3 * n, 3)].reshape(192, 512)
                part = jnp.dot(rows, wall[g, 2048 + 512 * b:2560 + 512 * b, :], preferred_element_type=F32)
                total = part if total is None else total + part
            res[g, pl.ds(3 * n, 3)] = total.astype(BF).reshape(3, 64, 256)

        loop(0, 2, project)

        def b_send(i):
            other = lax.rem(j + i, 8)

            @pl.when(has_span(other, z))
            def _():
                b_copy(g, j, other).start()

        loop(1, 8, b_send)

    def c_local(g, source, k):
        return pltpu.make_async_copy(ob.at[g, source], fb.at[k], lsem.at[0])

    def c_send(g, source):
        to = source + 8 * g
        k = span_of(j, z)

        @pl.when(to == z)
        def _():
            c_local(g, source, k).start()

        @pl.when(to != z)
        def _():
            remote(ob.at[g, source], fb.at[k], cs.at[to], cr.at[k], dp, to).start()

    @pl.when(has_span(j, z))
    def _():
        for g in (0, 1):
            ob[g, j] = res[g, slot_of(j, z)]
            c_send(g, j)

            def relay(i):
                other = lax.rem(j + i, 8)
                b_copy(g, other, j).wait_recv()
                c_send(g, other)

            loop(1, 8, relay)
        c_local(0, 0, 0).wait()

    load_hid.wait()

    def land(k):
        @pl.when(plane_of(j, k) != z)
        def _():
            remote(ob.at[0, 0], fb.at[k], cs.at[0], cr.at[k], dp, z).wait_recv()

        out_ref[k] = (hid_ref[k].astype(F32) + fb[k].astype(F32)).astype(BF)

    loop(0, 12, land)

    def sent(k):
        p, copy = n_copy(k)
        _, copy_q = q_copy(k)

        @pl.when(p != z)
        def _():
            copy.wait_send()
            copy_q.wait_send()

    loop(0, 12, sent)

    def sent_dp(i):
        other = lax.rem(dp + i, 32)
        req_copy(dp, other).wait_send()
        reply(dp, other).wait_send()

    loop(1, 32, sent_dp)

    def sent_w(i):
        wz(s, i, right, 0).wait_send()

        @pl.when(e == 0)
        def _():
            wz(s, i, left, 1).wait_send()

        @pl.when(e >= 2)
        def _():
            wz(1 - s, i, left, 1).wait_send()

        for h in (0, 1):
            wx(h, i, 0).wait_send()
            wx(h, i, 1).wait_send()
            wf(h, i, 0).wait_send()

    loop(0, NP, sent_w)

    def b_sent(i):
        other = lax.rem(j + i, 8)

        @pl.when(has_span(other, z))
        def _():
            b_copy(0, j, other).wait_send()
            b_copy(1, j, other).wait_send()

    loop(1, 8, b_sent)

    @pl.when(has_span(j, z))
    def _():
        def c_sent(i):
            to = lax.rem(z + i, 16)
            remote(ob.at[0, 0], fb.at[0], cs.at[to], cr.at[0], dp, to).wait_send()

        loop(1, 16, c_sent)


def layer(owners, slots, db, queries, w_key, w_value, w_out, hidden):
    dma = pltpu.SemaphoreType.DMA
    any_ = pl.BlockSpec(memory_space=pl.ANY)
    vmem = pl.BlockSpec(memory_space=pltpu.VMEM)
    return pl.pallas_call(
        layer_kernel,
        name="layer",
        out_shape=jax.ShapeDtypeStruct((12, 64, 256), BF),
        in_specs=[vmem, vmem, any_, any_, any_, any_, any_, any_],
        out_specs=vmem,
        scratch_shapes=[
            pltpu.VMEM((256, 896), BF),
            pltpu.VMEM((12, 64, 256), BF),
            pltpu.VMEM((8, 128), jnp.int32),
            pltpu.VMEM((2, 8, 64, 256), BF),
            pltpu.VMEM((6, 2, 64, 256), BF),
            pltpu.VMEM((32, 8, 128), jnp.int32),
            pltpu.VMEM((32, 16, 896), BF),
            pltpu.VMEM((32, 16, 896), BF),
            pltpu.VMEM((12, 16, 896), BF),
            pltpu.VMEM((6, 16, 16, 896), BF),
            pltpu.VMEM((2, NP * 4 * PIECE, 256), BF),
            pltpu.VMEM((8, 6, 64, 512), BF),
            pltpu.VMEM((2, 6, 64, 256), BF),
            pltpu.VMEM((2, 8, 64, 256), BF),
            pltpu.VMEM((12, 64, 256), BF),
            dma((32,)), dma((32,)),
            dma((12,)), dma((16,)),
            dma((8,)), dma((8,)),
            dma((32,)), dma((32,)),
            dma((12,)), dma((16,)),
            dma((7, 2)), dma((8, 2)),
            dma((NP,)),
            dma((2, NP)), dma((2, NP)),
            dma((2, 2, NP)), dma((2, 2, NP)),
            dma((2, NP)), dma((2, NP)),
            dma((7, 2)), dma((8, 2)),
            dma((2, 8)), dma((2, 8)),
            dma((16,)), dma((12,)),
            dma((4,)), dma((2,)),
        ],
        compiler_params=pltpu.CompilerParams(
            collective_id=0, has_side_effects=True, vmem_limit_bytes=62 * 2**20
        ),
    )(owners, slots, db, queries, w_key, w_value, w_out, hidden)


def per_device(hidden, queries, database, w_key, w_value, w_out, owners, entry_slots):
    mixed = layer(
        owners.T, entry_slots.T, database.reshape(256, 896), queries.reshape(12, 64, 256),
        w_key, w_value, w_out, hidden.reshape(12, 64, 256),
    )
    return mixed.reshape(768, 256)


def solution(mesh):
    in_specs = (
        P("dp", "tensor"),
        P("dp", "tensor"),
        P("dp", "tensor", None),
        P(None, "tensor"),
        P(None, "tensor"),
        P(None, "tensor"),
        P("dp", None),
        P("dp", None),
    )
    return jax.shard_map(
        per_device, mesh=mesh, in_specs=in_specs, out_specs=P("dp", "tensor"), check_vma=False
    )
```
